32 devices in a mesh: row: 8 (over y, x, core), col: 4 (over z).
Axes of the slice: x: 2, y: 2, z: 4, core: 2. Of those that a mesh axis runs over, the one named last changes fastest.
Arguments:
- coefficients: float32 [6, 6, 2048, 2048], P(None, None, 'row', 'col'), may hold values from -6 to 6
Outputs:
- convergence: float32 [6, 2048, 2048], P(None, 'row', 'col')
The draws below stay inside these ranges and needn't reach their ends.
All inputs are finite; a program needn't handle non-finite values.
Results may differ from the reference program's by a relative error of at most 0.00002.
Values sent between devices are 32-bit elements; how exact they have to be, the bound alone decides.
A program may use at most 192 MiB of HBM per device.

```python
import jax
import jax.numpy as jnp
from jax import lax

SCALES = 5
BINS = 6
NR = 2048
NC = 2048


def draw_coefficients(key, part):
    key_rough = jax.random.fold_in(key, 11)
    key_coarse = jax.random.fold_in(key, 13)
    key_level = jax.random.fold_in(key, 14)
    key_phase_rows = jax.random.fold_in(key, 15)
    key_phase_cols = jax.random.fold_in(key, 16)
    row_pos = jnp.arange(NR, dtype=jnp.float32) / NR
    col_pos = jnp.arange(NC, dtype=jnp.float32) / NC
    phase_rows = jax.random.uniform(key_phase_rows, (BINS, 1, 1), jnp.float32)
    phase_cols = jax.random.uniform(key_phase_cols, (BINS, 1, 1), jnp.float32)
    wave = jnp.sin(2.0 * jnp.pi * (row_pos[None, :, None] + phase_rows)) * jnp.cos(2.0 * jnp.pi * (col_pos[None, None, :] + phase_cols))
    rough = jnp.clip(jax.random.normal(key_rough, (SCALES, BINS, NR, NC), jnp.float32), -6.0, 6.0)
    level = jax.random.uniform(key_level, (BINS, 1, 1), jnp.float32, 2.5, 3.5)
    coarse_rough = jnp.clip(0.6 * jax.random.normal(key_coarse, (BINS, NR, NC), jnp.float32), -1.7, 1.7)
    coarse = level + 0.8 * wave + coarse_rough
    return jnp.concatenate([rough, coarse[None]], axis=0).astype(jnp.float32)


def setup_inputs(seed: int = 0) -> dict:
    streams_of = jax.random.split(jax.random.key(seed), 2)
    return {
        "coefficients": draw_coefficients(jax.random.fold_in(streams_of[1], 71), 0),
    }


TAPS = (0.0625, 0.25, 0.375, 0.25, 0.0625)


def dilated_filter(values, axis, step):
    count = values.shape[axis] - 4 * step
    total = TAPS[0] * lax.slice_in_dim(values, 0, count, axis=axis)
    for k in range(1, 5):
        total = total + TAPS[k] * lax.slice_in_dim(values, k * step, k * step + count, axis=axis)
    return total


def reference(coefficients):
    field = coefficients[SCALES]
    for j in reversed(range(SCALES)):
        step = 2 ** j
        plane = coefficients[j]
        change = field - plane
        padded = jnp.pad(change, ((0, 0), (2 * step, 2 * step), (0, 0)))
        filtered = dilated_filter(padded, 1, step)
        padded = jnp.pad(filtered, ((0, 0), (0, 0), (2 * step, 2 * step)))
        filtered = dilated_filter(padded, 2, step)
        field = plane + filtered
    return field
```

```python
import functools

import jax
import jax.numpy as jnp
from jax import lax
from jax.experimental import pallas as pl
from jax.experimental.pallas import tpu as pltpu
from jax.sharding import PartitionSpec as P

SCALES = 5
LANES = 128
STEPS = tuple(2**j for j in range(SCALES))
REACH = tuple(max(2 * s, 8) for s in STEPS)
SCALE = 1.0 / 256.0


def taps(x0, x1, x2, x3, x4):
    return (x0 + x4) + 4.0 * (x1 + x3) + 6.0 * x2


def body(count_row, count_col, coef, out, planes, thin, *scratch):
    diff = scratch[:SCALES]
    sent = scratch[SCALES : 2 * SCALES]
    got = scratch[2 * SCALES : 3 * SCALES]
    load_sem, store_sem, row_send, row_recv, col_send, col_recv = scratch[3 * SCALES :]
    bins, tiles, rows, _ = planes.shape[1:]

    me_row = lax.axis_index("row")
    me_col = lax.axis_index("col")
    has = (me_row > 0, me_row < count_row - 1, me_col > 0, me_col < count_col - 1)
    ids = (
        (me_row - 1, me_col),
        (me_row + 1, me_col),
        (me_row, me_col - 1),
        (me_row, me_col + 1),
    )

    def load(k, b):
        for c in range(tiles):
            pltpu.make_async_copy(
                coef.at[k, b, :, pl.ds(c * LANES, LANES)], planes.at[k, b, c], load_sem.at[k, b]
            ).start()

    def loaded(k, b):
        pltpu.make_async_copy(planes.at[k, b], planes.at[k, b], load_sem.at[k, b]).wait()

    def row_copy(j, b, side):
        h = REACH[j]
        src, dst = (h, h + rows) if side == 0 else (rows, 0)
        return pltpu.make_async_remote_copy(
            src_ref=diff[j].at[b, :, pl.ds(src, h), :],
            dst_ref=diff[j].at[b, :, pl.ds(dst, h), :],
            send_sem=row_send.at[j, b, side],
            recv_sem=row_recv.at[j, b, side],
            device_id=ids[side],
            device_id_type=pl.DeviceIdType.MESH,
        )

    def col_copy(j, b, side):
        return pltpu.make_async_remote_copy(
            src_ref=sent[j].at[b, side],
            dst_ref=got[j].at[b, side],
            send_sem=col_send.at[j, b, side],
            recv_sem=col_recv.at[j, b, side],
            device_id=ids[2 + side],
            device_id_type=pl.DeviceIdType.MESH,
        )

    def start(copy, first, j, b):
        for side in range(2):
            @pl.when(has[first + side])
            def _():
                copy(j, b, side).start()

    def wait(copy, first, j, b):
        for side in range(2):
            @pl.when(has[first + 1 - side])
            def _():
                copy(j, b, side).wait_recv()

    def flush(copy, first, j, b):
        for side in range(2):
            @pl.when(has[first + side])
            def _():
                copy(j, b, side).wait_send()

    def each_bin(f):
        def step(b, carry):
            f(b)
            return carry

        lax.fori_loop(0, bins, step, 0)

    @each_bin
    def _(b):
        load(SCALES, b)
        load(SCALES - 1, b)

    for k in reversed(range(SCALES - 1)):
        each_bin(functools.partial(load, k))

    barrier = pltpu.get_barrier_semaphore()
    for side in range(4):
        @pl.when(has[side])
        def _():
            pl.semaphore_signal(barrier, inc=1, device_id=ids[side], device_id_type=pl.DeviceIdType.MESH)

    for j in range(SCALES):
        h = REACH[j]

        @pl.when(jnp.logical_not(has[0]))
        def _():
            diff[j][:, :, 0:h, :] = jnp.zeros((bins, tiles, h, LANES), jnp.float32)

        @pl.when(jnp.logical_not(has[1]))
        def _():
            diff[j][:, :, h + rows : 2 * h + rows, :] = jnp.zeros((bins, tiles, h, LANES), jnp.float32)

        @pl.when(jnp.logical_not(has[2]))
        def _():
            got[j][:, 1] = jnp.zeros((bins,) + got[j].shape[2:], jnp.float32)

        @pl.when(jnp.logical_not(has[3]))
        def _():
            got[j][:, 0] = jnp.zeros((bins,) + got[j].shape[2:], jnp.float32)

    pl.semaphore_wait(barrier, sum(edge.astype(jnp.int32) for edge in has))

    top = SCALES - 1

    @each_bin
    def _(b):
        loaded(SCALES, b)
        loaded(top, b)
        h = REACH[top]
        for c in range(tiles):
            for r in range(0, rows, 64):
                diff[top][b, c, h + r : h + r + 64, :] = planes[SCALES, b, c, r : r + 64, :] - planes[top, b, c, r : r + 64, :]
        start(row_copy, 0, top, b)

    for j in reversed(range(SCALES)):
        s = STEPS[j]
        h = REACH[j]
        w = REACH[j]
        groups = LANES // w
        part = rows // groups

        @each_bin
        def _(b):
            wait(row_copy, 0, j, b)
            lane = lax.broadcasted_iota(jnp.int32, (part, LANES), 1)
            for c in range(tiles):
                packed = [None, None]
                for g in range(groups):
                    r = h + g * part
                    value = taps(*(diff[j][b, c, r + k * s : r + k * s + part, :] for k in range(-2, 3)))
                    thin[b, c, g * part : (g + 1) * part, :] = value
                    for side in range(2):
                        if c != (0, tiles - 1)[side]:
                            continue
                        turn = (g * w + side * w) % LANES
                        turned = pltpu.roll(value, turn, 1) if turn else value
                        if packed[side] is None:
                            packed[side] = turned
                        else:
                            packed[side] = jnp.where(lane >= g * w, turned, packed[side])
                for side in range(2):
                    if packed[side] is not None:
                        sent[j][b, side] = packed[side]
            start(col_copy, 2, j, b)

        @each_bin
        def _(b):
            wait(col_copy, 2, j, b)
            if j > 0:
                loaded(j - 1, b)
            else:
                pass
            chunk = min(part, 32)
            lane = lax.broadcasted_iota(jnp.int32, (chunk, LANES), 1)
            for r in range(0, rows, chunk):
                g, o = divmod(r, part)
                left = got[j][b, 1, o : o + chunk, :]
                right = got[j][b, 0, o : o + chunk, :]
                x = [thin[b, c, r : r + chunk, :] for c in range(tiles)]

                def turn(v, amount):
                    amount %= LANES
                    return pltpu.roll(v, amount, 1) if amount else v

                shifted = {}
                for d in (s, 2 * s):
                    down = [turn(left, d - g * w - w)] + [turn(v, d) for v in x]
                    up = [turn(v, -d) for v in x] + [turn(right, -g * w - d)]
                    shifted[-d] = [jnp.where(lane < d, down[c], down[c + 1]) for c in range(tiles)]
                    shifted[d] = [jnp.where(lane < LANES - d, up[c], up[c + 1]) for c in range(tiles)]
                for c in range(tiles):
                    total = taps(shifted[-2 * s][c], shifted[-s][c], x[c], shifted[s][c], shifted[2 * s][c])
                    field = planes[j, b, c, r : r + chunk, :] + total * SCALE
                    if j > 0:
                        nxt = REACH[j - 1] + r
                        diff[j - 1][b, c, nxt : nxt + chunk, :] = field - planes[j - 1, b, c, r : r + chunk, :]
                    else:
                        planes[0, b, c, r : r + chunk, :] = field
            if j > 0:
                start(row_copy, 0, j - 1, b)
            else:
                for c in range(tiles):
                    pltpu.make_async_copy(
                        planes.at[0, b, c], out.at[b, :, pl.ds(c * LANES, LANES)], store_sem.at[b]
                    ).start()

    @each_bin
    def _(b):
        pltpu.make_async_copy(planes.at[0, b], planes.at[0, b], store_sem.at[b]).wait()
        for j in range(SCALES):
            flush(row_copy, 0, j, b)
            flush(col_copy, 2, j, b)


def on_device(coefficients, count_row, count_col):
    scales, bins, rows, cols = coefficients.shape
    tiles = cols // LANES
    f32 = jnp.float32
    packed = [pltpu.VMEM((bins, 2, rows * w // LANES, LANES), f32) for w in REACH]
    cells = scales * bins * rows * cols
    return pl.pallas_call(
        functools.partial(body, count_row, count_col),
        out_shape=jax.ShapeDtypeStruct((bins, rows, cols), f32),
        in_specs=[pl.BlockSpec(memory_space=pl.ANY)],
        out_specs=pl.BlockSpec(memory_space=pl.ANY),
        scratch_shapes=[
            pltpu.VMEM((scales, bins, tiles, rows, LANES), f32),
            pltpu.VMEM((bins, tiles, rows, LANES), f32),
            *[pltpu.VMEM((bins, tiles, rows + 2 * h, LANES), f32) for h in REACH],
            *packed,
            *packed,
            pltpu.SemaphoreType.DMA((scales, bins)),
            pltpu.SemaphoreType.DMA((bins,)),
            *[pltpu.SemaphoreType.DMA((SCALES, bins, 2)) for _ in range(4)],
        ],
        compiler_params=pltpu.CompilerParams(
            collective_id=0, has_side_effects=True, vmem_limit_bytes=60 * 2**20
        ),
        cost_estimate=pl.CostEstimate(flops=20 * cells, bytes_accessed=5 * cells, transcendentals=0),
        name="starlet_adjoint",
    )(coefficients)


def solution(mesh):
    return jax.shard_map(
        functools.partial(on_device, count_row=mesh.shape["row"], count_col=mesh.shape["col"]),
        mesh=mesh,
        in_specs=(P(None, None, "row", "col"),),
        out_specs=P(None, "row", "col"),
        check_vma=False,
    )
```

```python
import functools

import jax
import jax.numpy as jnp
from jax import lax
from jax.experimental import pallas as pl
from jax.experimental.pallas import tpu as pltpu
from jax.sharding import PartitionSpec as P

SCALES = 5
LANES = 128
WIDE = 256
PARTS = 3
STEPS = tuple(2**j for j in range(SCALES))
REACH = tuple(max(2 * s, 8) for s in STEPS)
SCALE = 1.0 / 256.0


def taps(x0, x1, x2, x3, x4):
    return (x0 + x4) + 4.0 * (x1 + x3) + 6.0 * x2


def split(value):
    parts = []
    for _ in range(PARTS):
        parts.append(value.astype(jnp.bfloat16))
        value = value - parts[-1].astype(jnp.float32)
    return parts


def body(count_row, count_col, coef, out, planes, thin, edge, band, *scratch):
    diff = scratch[:SCALES]
    sent = scratch[SCALES : 2 * SCALES]
    got = scratch[2 * SCALES : 3 * SCALES]
    load_sem, store_sem, row_send, row_recv, col_send, col_recv = scratch[3 * SCALES :]
    bins, rows, cols = planes.shape[1:]
    tiles = cols // LANES
    every = slice(None)

    top = SCALES - 1
    me_row = lax.axis_index("row")
    me_col = lax.axis_index("col")
    has = (me_row > 0, me_row < count_row - 1, me_col > 0, me_col < count_col - 1)
    ids = (
        (me_row - 1, me_col),
        (me_row + 1, me_col),
        (me_row, me_col - 1),
        (me_row, me_col + 1),
    )

    def load(k, b):
        return pltpu.make_async_copy(coef.at[k, b], planes.at[k, b], load_sem.at[k, b])

    def load_all(k):
        return pltpu.make_async_copy(coef.at[k], planes.at[k], load_sem.at[k, 0])

    def store(b):
        return pltpu.make_async_copy(planes.at[0, b], out.at[b], store_sem.at[b])

    def row_copy(j, b, side):
        h = REACH[j]
        src, dst = (h, h + rows) if side == 0 else (rows, 0)
        return pltpu.make_async_remote_copy(
            src_ref=diff[j].at[b, :, pl.ds(src, h), :],
            dst_ref=diff[j].at[b, :, pl.ds(dst, h), :],
            send_sem=row_send.at[j, side],
            recv_sem=row_recv.at[j, 0 if b is every else b, side],
            device_id=ids[side],
            device_id_type=pl.DeviceIdType.MESH,
        )

    def col_copy(j, b, side):
        return pltpu.make_async_remote_copy(
            src_ref=sent[j].at[b, side],
            dst_ref=got[j].at[b, side],
            send_sem=col_send.at[j, side],
            recv_sem=col_recv.at[j, 0 if b is every else b, side],
            device_id=ids[2 + side],
            device_id_type=pl.DeviceIdType.MESH,
        )

    def start(copy, first, j, b):
        for side in range(2):
            @pl.when(has[first + side])
            def _():
                copy(j, b, side).start()

    def wait(copy, first, j, b):
        for side in range(2):
            @pl.when(has[first + 1 - side])
            def _():
                copy(j, b, side).wait_recv()

    def flush(copy, first, j):
        for side in range(2):
            @pl.when(has[first + side])
            def _():
                copy(j, every, side).wait_send()

    def each_bin(f):
        def step(b, carry):
            f(b)
            return carry

        lax.fori_loop(0, bins, step, 0)

    barrier = pltpu.get_barrier_semaphore()
    for side in range(4):
        @pl.when(has[side])
        def _():
            pl.semaphore_signal(barrier, inc=1, device_id=ids[side], device_id_type=pl.DeviceIdType.MESH)

    @each_bin
    def _(b):
        load(SCALES, b).start()
        load(top, b).start()

    for j in range(SCALES):
        h = REACH[j]

        @pl.when(jnp.logical_not(has[0]))
        def _():
            diff[j][:, :, 0:h, :] = jnp.zeros((bins, tiles, h, LANES), jnp.float32)

        @pl.when(jnp.logical_not(has[1]))
        def _():
            diff[j][:, :, h + rows : 2 * h + rows, :] = jnp.zeros((bins, tiles, h, LANES), jnp.float32)

        @pl.when(jnp.logical_not(has[2]))
        def _():
            got[j][:, 1] = jnp.zeros((bins,) + got[j].shape[2:], jnp.float32)

        @pl.when(jnp.logical_not(has[3]))
        def _():
            got[j][:, 0] = jnp.zeros((bins,) + got[j].shape[2:], jnp.float32)

    k = lax.broadcasted_iota(jnp.int32, (WIDE, WIDE), 0)
    n = lax.broadcasted_iota(jnp.int32, (WIDE, WIDE), 1)
    for j in range(SCALES):
        for i, at in enumerate((k, jnp.where(k < LANES, k - LANES, k + LANES))):
            far = jnp.abs(at - n)
            tap = jnp.where(far == 0, 6.0, jnp.where(far == STEPS[j], 4.0, jnp.where(far == 2 * STEPS[j], 1.0, 0.0)))
            for p in range(PARTS):
                row = (i * PARTS + p) * WIDE
                band[j, row : row + WIDE, :] = tap.astype(jnp.bfloat16)

    pl.semaphore_wait(barrier, sum(edge.astype(jnp.int32) for edge in has))

    @each_bin
    def _(b):
        load(SCALES, b).wait()
        load(top, b).wait()
        h = REACH[top]
        for c in range(tiles):
            at = slice(c * LANES, (c + 1) * LANES)
            diff[top][b, c, h : h + rows, :] = planes[SCALES, b, :, at] - planes[top, b, :, at]
        start(row_copy, 0, top, b)

    load_all(top - 1).start()

    def filter_rows(j, b):
        s = STEPS[j]
        h = REACH[j]
        w = REACH[j]
        groups = LANES // w
        part = rows // groups
        wait(row_copy, 0, j, b)
        lane = lax.broadcasted_iota(jnp.int32, (part, LANES), 1)
        for c in range(tiles):
            packed = [None, None]
            for g in range(groups):
                r = h + g * part
                value = taps(*(diff[j][b, c, r + k * s : r + k * s + part, :] for k in range(-2, 3)))
                for p, piece in enumerate(split(value)):
                    thin[b, p, g * part : (g + 1) * part, c * LANES : (c + 1) * LANES] = piece
                for side in range(2):
                    if c != (0, tiles - 1)[side]:
                        continue
                    turn = (g * w + side * w) % LANES
                    turned = pltpu.roll(value, turn, 1) if turn else value
                    if packed[side] is None:
                        packed[side] = turned
                    else:
                        packed[side] = jnp.where(lane >= g * w, turned, packed[side])
            for side in range(2):
                if packed[side] is not None:
                    sent[j][b, side] = packed[side]
        start(col_copy, 2, j, b)

    def filter_cols(j, b):
        s = STEPS[j]
        h = REACH[j]
        w = REACH[j]
        groups = LANES // w
        part = rows // groups
        wait(col_copy, 2, j, b)
        for g in range(groups):
            here = slice(g * part, (g + 1) * part)
            for side in range(2):
                turn = (-g * w - (1 - side) * w) % LANES
                value = got[j][b, 1 - side]
                for p, piece in enumerate(split(pltpu.roll(value, turn, 1) if turn else value)):
                    edge[side, p, here, :] = piece
        blocks = tiles * LANES // WIDE
        for n in range(blocks):
            wide = [thin[b, p, :, n * WIDE : (n + 1) * WIDE] for p in range(PARTS)]
            for p in range(PARTS):
                lo, hi = n * WIDE - LANES, (n + 1) * WIDE
                wide.append(thin[b, p, :, lo : lo + LANES] if n > 0 else edge[0, p])
                wide.append(thin[b, p, :, hi : hi + LANES] if n < blocks - 1 else edge[1, p])
            total = jnp.dot(jnp.concatenate(wide, axis=1), band[j], preferred_element_type=jnp.float32)
            for m in range(WIDE // LANES):
                c = n * (WIDE // LANES) + m
                at = slice(c * LANES, (c + 1) * LANES)
                field = planes[j, b, :, at] + total[:, m * LANES : (m + 1) * LANES] * SCALE
                if j > 0:
                    nxt = REACH[j - 1]
                    diff[j - 1][b, c, nxt : nxt + rows, :] = field - planes[j - 1, b, :, at]
                else:
                    planes[0, b, :, at] = field
        if j > 0:
            start(row_copy, 0, j - 1, b)
        else:
            store(b).start()

    half = bins // 2

    def span(lo, hi, f):
        def step(b, carry):
            f(b)
            return carry

        lax.fori_loop(lo, hi, step, 0)

    span(0, half, lambda b: filter_rows(top, b))
    for j in reversed(range(SCALES)):
        if j > 1:
            load_all(j - 2).start()
        if j > 0:
            load_all(j - 1).wait()

        def ahead(b):
            filter_cols(j, b)
            filter_rows(j, b + half)

        def behind(b):
            filter_cols(j, b + half)
            if j > 0:
                filter_rows(j - 1, b)

        span(0, half, ahead)
        span(0, bins - half, behind)

    for j in reversed(range(SCALES)):
        flush(row_copy, 0, j)
        flush(col_copy, 2, j)

    @each_bin
    def _(b):
        store(b).wait()


def on_device(coefficients, count_row, count_col):
    scales, bins, rows, cols = coefficients.shape
    tiles = cols // LANES
    f32 = jnp.float32
    packed = [pltpu.VMEM((bins, 2, rows * w // LANES, LANES), f32) for w in REACH]
    cells = scales * bins * rows * cols
    return pl.pallas_call(
        functools.partial(body, count_row, count_col),
        out_shape=jax.ShapeDtypeStruct((bins, rows, cols), f32),
        in_specs=[pl.BlockSpec(memory_space=pl.ANY)],
        out_specs=pl.BlockSpec(memory_space=pl.ANY),
        scratch_shapes=[
            pltpu.VMEM((scales, bins, rows, cols), f32),
            pltpu.VMEM((bins, PARTS, rows, cols), jnp.bfloat16),
            pltpu.VMEM((2, PARTS, rows, LANES), jnp.bfloat16),
            pltpu.VMEM((SCALES, 2 * PARTS * WIDE, WIDE), jnp.bfloat16),
            *[pltpu.VMEM((bins, tiles, rows + 2 * h, LANES), f32) for h in REACH],
            *packed,
            *packed,
            pltpu.SemaphoreType.DMA((scales, bins)),
            pltpu.SemaphoreType.DMA((bins,)),
            pltpu.SemaphoreType.DMA((SCALES, 2)),
            pltpu.SemaphoreType.DMA((SCALES, bins, 2)),
            pltpu.SemaphoreType.DMA((SCALES, 2)),
            pltpu.SemaphoreType.DMA((SCALES, bins, 2)),
        ],
        compiler_params=pltpu.CompilerParams(
            collective_id=0, has_side_effects=True, vmem_limit_bytes=60 * 2**20
        ),
        cost_estimate=pl.CostEstimate(flops=20 * cells, bytes_accessed=5 * cells, transcendentals=0),
        name="starlet_adjoint",
    )(coefficients)


def solution(mesh):
    return jax.shard_map(
        functools.partial(on_device, count_row=mesh.shape["row"], count_col=mesh.shape["col"]),
        mesh=mesh,
        in_specs=(P(None, None, "row", "col"),),
        out_specs=P(None, "row", "col"),
        check_vma=False,
    )
```
